256 devices in a mesh: depth: 4 (over x_hi, core), tile: 64 (over x_lo, y, z).
Axes of the slice: x: 4 (x_hi: 2, x_lo: 2; x = x_hi * 2 + x_lo), y: 4, z: 8, core: 2. Of those that a mesh axis runs over, the one named last changes fastest.
Arguments:
- incident: float32 [2, 3, 2048, 512], P(None, None, 'tile'), may hold values from -6 to 6
- delta: float32 [3, 8, 2048, 512], P(None, 'depth', 'tile'), may hold values from 0 to 1
- beta: float32 [3, 8, 2048, 512], P(None, 'depth', 'tile'), may hold values from 0 to 0.5
- view_order: int32 [3], replicated, may hold values from 0 to 2, each once
Outputs:
- slab_waves: float32 [2, 3, 4, 2048, 512], P(None, None, 'depth', 'tile')
The draws below stay inside these ranges and needn't reach their ends.
Inputs may be any that keep to these rules, and one draw needn't show every extreme that they name: `view_order`: each view appears once.
All inputs are finite; a program needn't handle non-finite values.
Results may differ from the reference program's by a relative error of at most 0.0001.
Values sent between devices are 32-bit elements; how exact they have to be, the bound alone decides.
No kernel may reach another device: no remote copies, remote signals or barrier semaphores. Data moves between devices by JAX's collectives and lax.ppermute only.
A program may use at most 64 MiB of HBM per device.

```python
import jax
import jax.numpy as jnp
from jax import lax

VIEWS = 3
SLAB = 2
HALF = 32
COLS = 512
NX = 2048
SLICES = 8


def block_scale(key, dims, split, least, top_value):
    level = 1.0
    for position, blocks in split:
        heights = jax.random.uniform(jax.random.fold_in(jax.random.fold_in(key, 6), position), (blocks,), jnp.float32, least / len(split), top_value / len(split))
        level = level * jnp.repeat(jnp.exp(heights), dims[position] // blocks).reshape((-1,) + (1,) * (len(dims) - 1 - position))
    return level


def centred(stream_key, shape, scale, bound, pieces=(), held_as=jnp.bfloat16):
    drawn = scale * jax.random.normal(stream_key, shape, jnp.float32)
    if pieces:
        drawn = drawn * block_scale(stream_key, shape, pieces, -0.22, 0.18)
    return jnp.clip(drawn, -bound, bound).astype(held_as)


def setup_inputs(seed: int = 0) -> dict:
    arg_keys = jax.random.split(jax.random.key(seed), 5)
    return {
        "incident": centred(arg_keys[0], (2, VIEWS, NX, COLS), 1.0, 6.0, ((2, 64),), jnp.float32),
        "delta": jnp.clip(1.0 * jax.random.uniform(arg_keys[1], (VIEWS, SLICES, NX, COLS), jnp.float32) ** block_scale(arg_keys[1], (VIEWS, SLICES, NX, COLS), ((1, 4), (2, 64)), -0.2, 0.2), 0.0, 1.0),
        "beta": jnp.clip(0.5 * jax.random.uniform(arg_keys[2], (VIEWS, SLICES, NX, COLS), jnp.float32) ** block_scale(arg_keys[2], (VIEWS, SLICES, NX, COLS), ((1, 4), (2, 64)), -0.2, 0.2), 0.0, 0.5),
        "view_order": jax.random.permutation(arg_keys[3], VIEWS).astype(jnp.int32),
    }


def tap_table(half):
    grid = jnp.arange(-half, half + 1).astype(jnp.float32)
    window = 0.75 + 0.25 * jnp.cos(jnp.pi * grid / (half + 1))
    angle = jnp.pi * grid * grid / (6.25 * half)
    real_part = window * jnp.cos(angle)
    imag_part = window * jnp.sin(angle)
    norm = jnp.sqrt(jnp.sum(real_part) ** 2 + jnp.sum(imag_part) ** 2)
    return (real_part / norm, imag_part / norm)

def convolve(field, taps_re, taps_im, along_rows):
    kernel = jnp.stack([jnp.stack([taps_re, -taps_im]), jnp.stack([taps_im, taps_re])])
    if along_rows:
        kernel = kernel[:, :, :, None]
        padding = ((HALF, HALF), (0, 0))
    else:
        kernel = kernel[:, :, None, :]
        padding = ((0, 0), (HALF, HALF))
    result = lax.conv_general_dilated(field[None], kernel.astype(field.dtype), (1, 1), padding, dimension_numbers=('NCHW', 'OIHW', 'NCHW'), precision=lax.Precision.HIGHEST)
    return result[0]

def reference(incident, delta, beta, view_order):
    taps_re, taps_im = tap_table(HALF)
    stored = []
    for slot in range(VIEWS):
        view = view_order[slot]
        field = jnp.take(incident, view, axis=1)
        slabs = []
        for piece in range(SLICES):
            amp = jnp.exp(-jnp.take(beta, view, axis=0)[piece])
            phase = -jnp.pi * jnp.take(delta, view, axis=0)[piece]
            trans_re = amp * jnp.cos(phase)
            trans_im = amp * jnp.sin(phase)
            field = jnp.stack([field[0] * trans_re - field[1] * trans_im, field[0] * trans_im + field[1] * trans_re])
            field = convolve(field, taps_re, taps_im, True)
            field = convolve(field, taps_re, taps_im, False)
            if piece % SLAB == SLAB - 1:
                slabs.append(field)
        stored.append(jnp.stack(slabs, axis=1))
    return jnp.stack(stored, axis=1)
```

```python
import jax
import jax.numpy as jnp
import numpy as np
from jax import lax
from jax.experimental import pallas as pl
from jax.experimental.pallas import tpu as pltpu
from jax.sharding import PartitionSpec as P

HALF = 32
ROWS = 32
COLS = 512
LANES = 128
VIEWS = 3
SLABS = 4
TILES = 64
AXES = ("depth", "tile")
USE_KERNELS = True


def device_at(x, y, z, core):
    return ((x // 2) * 2 + core) * TILES + (x % 2) * 32 + y * 8 + z


def worker(slot, tile):
    chip, core = divmod(tile, 2)
    x_lo, rest = divmod(chip, 16)
    y, z = divmod(rest, 4)
    z = z if y % 2 == 0 else 3 - z
    y = y if x_lo == 0 else 3 - y
    return device_at(2 * (slot // 2) + x_lo, y, z + 4 * (slot % 2), core)


def home(depth, tile):
    return depth * TILES + tile


INNER = [(worker(k, p), worker(k, p ^ 1)) for k in range(4) for p in range(TILES)]
OUTER = [
    (worker(k, p), worker(k, (p + 1) % TILES if p % 2 else (p - 1) % TILES))
    for k in range(4)
    for p in range(TILES)
]


def taps():
    grid = np.arange(-HALF, HALF + 1).astype(np.float64)
    value = (0.75 + 0.25 * np.cos(np.pi * grid / (HALF + 1))) * np.exp(1j * np.pi * grid * grid / (6.25 * HALF))
    return value / np.abs(value.sum())


def tap_at(offset):
    table = taps()
    inside = np.abs(offset) <= HALF
    return np.where(inside, table[np.clip(offset + HALF, 0, 2 * HALF)], 0.0)


def halves(matrix):
    matrix = jnp.asarray(matrix.astype(np.float32))
    high = matrix.astype(jnp.bfloat16)
    low = (matrix - high.astype(jnp.float32)).astype(jnp.bfloat16)
    return high, low


def column_matrix():
    source = np.arange(3 * LANES)[:, None] - LANES
    target = np.arange(LANES)[None, :]
    value = tap_at(source - target)
    return np.concatenate([value.real, value.imag], axis=1)


def row_block(shift):
    target = np.arange(ROWS)[:, None]
    source = np.arange(ROWS)[None, :] + shift
    value = tap_at(source - target)
    return np.block([[value.real, -value.imag], [value.imag, value.real]])


def row_matrix(parity):
    low, mid, high = row_block(-ROWS), row_block(0), row_block(ROWS)
    first, last = (low, high) if parity else (high, low)
    return np.concatenate([first, mid, last], axis=1)


def split(value):
    high = value.astype(jnp.bfloat16)
    return high, (value - high.astype(jnp.float32)).astype(jnp.bfloat16)


def dot(a, b):
    return jnp.dot(a, b, preferred_element_type=jnp.float32)


def row_blur(inner, own, outer, rhi, rlo):
    high, low = split(jnp.concatenate([inner, own, outer], axis=0))
    return dot(rhi, high) + (dot(rlo, high) + dot(rhi, low))


def column_blur(field, chi, clo):
    high, low = split(field)
    parts = []
    for b in range(COLS // LANES):
        first, last = max(0, b - 1), min(COLS // LANES, b + 2)
        cols = slice(first * LANES, last * LANES)
        rows = slice((first - b + 1) * LANES, (last - b + 1) * LANES)
        h, l = high[:, cols], low[:, cols]
        ch, cl = chi[rows], clo[rows]
        out = dot(h, ch) + (dot(l, ch) + dot(h, cl))
        real = out[:ROWS, :LANES] - out[ROWS:, LANES:]
        imag = out[:ROWS, LANES:] + out[ROWS:, :LANES]
        parts.append(jnp.concatenate([real, imag], axis=0))
    return jnp.concatenate(parts, axis=1)


def times(trans, field):
    tr, ti = trans[:ROWS], trans[ROWS:]
    fr, fi = field[:ROWS], field[ROWS:]
    return jnp.concatenate([fr * tr - fi * ti, fr * ti + fi * tr], axis=0)


def sin_poly(x):
    s = x * x
    p = -2.5052108385441720e-08
    for c in (2.7557319223985893e-06, -1.9841269841269841e-04, 8.3333333333333333e-03, -1.6666666666666667e-01):
        p = p * s + c
    return x + x * (s * p)


def cos_poly(x):
    s = x * x
    p = 2.0876756987868099e-09
    for c in (-2.7557319223985888e-07, 2.4801587301587302e-05, -1.3888888888888889e-03, 4.1666666666666667e-02, -0.5):
        p = p * s + c
    return 1.0 + s * p


def transmission(delta, beta):
    turn = (delta - 0.5) * np.float32(np.pi)
    amp = jnp.exp(-beta)
    return jnp.concatenate([-amp * sin_poly(turn), -amp * cos_poly(turn)], axis=0)


def pick(index, values):
    out = values[0]
    for i in range(1, len(values)):
        out = jnp.where(index == i, values[i], out)
    return out


def prepare_kernel(order, incident, delta, beta, *outs):
    depth = order[3]
    for slot in range(VIEWS):
        view = order[slot]
        even = transmission(delta[view, 0], beta[view, 0])
        odd = transmission(delta[view, 1], beta[view, 1])
        entering = jnp.concatenate([incident[0, view], incident[1, view]], axis=0)
        outs[slot][...] = times(even, entering)
        outs[VIEWS + slot][...] = odd
        place = lax.rem(depth + 5 - slot, 3)
        outs[2 * VIEWS][place, 0] = even
        outs[2 * VIEWS][place, 1] = odd


def first_kernel(a, b, c, chi, clo, out):
    out[...] = column_blur(a[...] + b[...] + c[...], chi[...], clo[...])


def middle_kernel(slab_end, n_trans, which, inner, own, outer, *refs):
    trans = refs[:n_trans]
    rhi, rlo, chi, clo = refs[n_trans : n_trans + 4]
    outs = refs[n_trans + 4 :]
    field = row_blur(inner[...], own[...], outer[...], rhi[...], rlo[...])
    if slab_end:
        outs[1][...] = field
    t = pick(which[0], [r[...] for r in trans])
    outs[0][...] = column_blur(times(t, field), chi[...], clo[...])


def last_kernel(inner, own, outer, rhi, rlo, out):
    out[...] = row_blur(inner[...], own[...], outer[...], rhi[...], rlo[...])


FIELD = jax.ShapeDtypeStruct((2 * ROWS, COLS), jnp.float32)


def call(kernel, out_shape, args, name, scalar_first=False):
    vmem = pl.BlockSpec(memory_space=pltpu.VMEM)
    smem = pl.BlockSpec(memory_space=pltpu.SMEM)
    specs = [smem if scalar_first and i == 0 else vmem for i in range(len(args))]
    outs = jax.tree.map(lambda _: vmem, out_shape)
    return pl.pallas_call(
        kernel, out_shape=out_shape, in_specs=specs, out_specs=outs, name=name, interpret=not USE_KERNELS
    )(*args)


def permute(value, pairs):
    return lax.ppermute(value, AXES, pairs)


def per_device(incident, delta, beta, view_order):
    depth, tile = lax.axis_index("depth"), lax.axis_index("tile")
    core = depth % 2
    slot = (depth // 2) * 2 + (tile % 8) // 4

    chi, clo = halves(column_matrix())
    even, odd = row_matrix(0), row_matrix(1)
    edge = jnp.logical_or(
        jnp.logical_and(core == 0, tile % 32 // 8 + tile // 32 * 4 + tile % 4 == 0),
        jnp.logical_and(core == 1, jnp.logical_and(tile // 32 == 1, tile % 32 // 8 + tile % 4 == 0)),
    )
    keep = jnp.logical_or(jnp.logical_not(edge), jnp.arange(6 * ROWS)[None, :] < 4 * ROWS)
    (ehi, elo), (ohi, olo) = halves(even), halves(odd)
    rhi = jnp.where(keep, jnp.where(core == 0, ehi, ohi), 0)
    rlo = jnp.where(keep, jnp.where(core == 0, elo, olo), 0)

    scalars = jnp.concatenate([view_order, depth[None]])
    pair = jax.ShapeDtypeStruct((VIEWS, 2) + FIELD.shape, jnp.float32)
    sent = call(
        prepare_kernel, [FIELD] * (2 * VIEWS) + [pair], (scalars, incident, delta, beta), "prepare", scalar_first=True
    )
    entering, second, rest = sent[:VIEWS], sent[VIEWS : 2 * VIEWS], sent[2 * VIEWS]

    def from_first(values):
        return [
            permute(values[k], [(home(0, p), worker(k, p)) for p in range(TILES)]) for k in range(VIEWS)
        ]

    starts = from_first(entering)
    seconds = from_first(second)
    later = [
        permute(
            rest[m],
            [(home(1 + (m + k) % 3, p), worker(k, p)) for k in range(VIEWS) for p in range(TILES)],
        )
        for m in range(3)
    ]

    own = call(first_kernel, FIELD, (*starts, chi, clo), "enter")
    slabs = []
    for piece in range(2 * SLABS):
        inner = permute(own, INNER)
        outer = permute(own, OUTER)
        if piece == 2 * SLABS - 1:
            slabs.append(call(last_kernel, FIELD, (inner, own, outer, rhi, rlo), "leave"))
            break
        nxt = piece + 1
        if nxt == 1:
            trans = list(seconds)
            which = jnp.minimum(slot, 2)[None]
        else:
            trans = [v[nxt % 2] for v in later]
            which = ((nxt // 2 + 5 - jnp.minimum(slot, 2)) % 3)[None]
        slab_end = piece % 2 == 1
        outs = call(
            lambda *refs, slab_end=slab_end, n=len(trans): middle_kernel(slab_end, n, *refs),
            [FIELD] * (2 if slab_end else 1),
            (which, inner, own, outer, *trans, rhi, rlo, chi, clo),
            "slice",
            scalar_first=True,
        )
        own = outs[0]
        if slab_end:
            slabs.append(outs[1])

    early = [
        permute(
            pick((slot + n) % 3, slabs[:3]),
            [(worker(k, p), home((n + k) % 3, p)) for k in range(VIEWS) for p in range(TILES)],
        )
        for n in range(3)
    ]
    last = [permute(slabs[3], [(worker(k, p), home(3, p)) for p in range(TILES)]) for k in range(VIEWS)]
    stored = [jnp.where(depth == 3, last[k], pick((depth + 3 - k) % 3, early)) for k in range(VIEWS)]
    return jnp.stack([v.reshape(2, ROWS, COLS) for v in stored], axis=1)[:, :, None]


def solution(mesh):
    return jax.shard_map(
        per_device,
        mesh=mesh,
        in_specs=(
            P(None, None, "tile", None),
            P(None, "depth", "tile", None),
            P(None, "depth", "tile", None),
            P(),
        ),
        out_specs=P(None, None, "depth", "tile", None),
        check_vma=False,
    )
```

```python
import functools

import jax
import jax.numpy as jnp
import numpy as np
from jax import lax
from jax.experimental import pallas as pl
from jax.experimental.pallas import tpu as pltpu
from jax.sharding import PartitionSpec as P

HALF = 32
ROWS = 32
COLS = 512
LANES = 128
VIEWS = 3
SLABS = 4
TILES = 64
AXES = ("depth", "tile")


def device_at(x, y, z, core):
    return ((x // 2) * 2 + core) * TILES + (x % 2) * 32 + y * 8 + z


def worker(slot, tile):
    x_lo, rest = divmod(tile, 32)
    y, z = divmod(rest, 8)
    y = y if x_lo == 0 else 3 - y
    core = 0 if z // 4 == slot % 2 else 1
    return device_at(2 * (slot // 2) + x_lo, y, z if core == 0 else 7 - z, core)


def home(depth, tile):
    return depth * TILES + tile


INNER = [(worker(k, p), worker(k, p ^ 1)) for k in range(4) for p in range(TILES)]
OUTER = [
    (worker(k, p), worker(k, (p + 1 if p % 2 else p - 1) % TILES))
    for k in range(4)
    for p in range(TILES)
]


def taps():
    grid = np.arange(-HALF, HALF + 1).astype(np.float64)
    value = (0.75 + 0.25 * np.cos(np.pi * grid / (HALF + 1))) * np.exp(1j * np.pi * grid * grid / (6.25 * HALF))
    return value / np.abs(value.sum())


def tap_at(offset):
    table = taps()
    inside = np.abs(offset) <= HALF
    return np.where(inside, table[np.clip(offset + HALF, 0, 2 * HALF)], 0.0)


def halves(matrix):
    matrix = jnp.asarray(matrix.astype(np.float32))
    high = matrix.astype(jnp.bfloat16)
    low = (matrix - high.astype(jnp.float32)).astype(jnp.bfloat16)
    return high, low


def column_matrix():
    source = np.arange(3 * LANES)[:, None] - LANES
    target = np.arange(LANES)[None, :]
    value = tap_at(source - target)
    return np.concatenate([value.real, value.imag], axis=1)


def row_block(shift):
    target = np.arange(ROWS)[:, None]
    source = np.arange(ROWS)[None, :] + shift
    value = tap_at(source - target)
    return np.block([[value.real, -value.imag], [value.imag, value.real]])


def row_matrix(parity):
    low, mid, high = row_block(-ROWS), row_block(0), row_block(ROWS)
    first, last = (low, high) if parity else (high, low)
    return np.concatenate([first, mid, last], axis=1)


def split(value):
    high = value.astype(jnp.bfloat16)
    return high, (value - high.astype(jnp.float32)).astype(jnp.bfloat16)


def dot(a, b):
    return jnp.dot(a, b, preferred_element_type=jnp.float32)


def row_blur(inner, own, outer, rhi, rlo):
    high, low = split(jnp.concatenate([inner, own, outer], axis=0))
    return dot(rhi, high) + (dot(rlo, high) + dot(rhi, low))


def column_blur(field, chi, clo):
    high, low = split(field)
    parts = []
    for b in range(COLS // LANES):
        first, last = max(0, b - 1), min(COLS // LANES, b + 2)
        cols = slice(first * LANES, last * LANES)
        rows = slice((first - b + 1) * LANES, (last - b + 1) * LANES)
        h, l = high[:, cols], low[:, cols]
        ch, cl = chi[rows], clo[rows]
        out = dot(h, ch) + (dot(l, ch) + dot(h, cl))
        real = out[:ROWS, :LANES] - out[ROWS:, LANES:]
        imag = out[:ROWS, LANES:] + out[ROWS:, :LANES]
        parts.append(jnp.concatenate([real, imag], axis=0))
    return jnp.concatenate(parts, axis=1)


def times(trans, field):
    tr, ti = trans[:ROWS], trans[ROWS:]
    fr, fi = field[:ROWS], field[ROWS:]
    return jnp.concatenate([fr * tr - fi * ti, fr * ti + fi * tr], axis=0)


def sin_poly(x):
    s = x * x
    p = -2.5052108385441720e-08
    for c in (2.7557319223985893e-06, -1.9841269841269841e-04, 8.3333333333333333e-03, -1.6666666666666667e-01):
        p = p * s + c
    return x + x * (s * p)


def cos_poly(x):
    s = x * x
    p = 2.0876756987868099e-09
    for c in (-2.7557319223985888e-07, 2.4801587301587302e-05, -1.3888888888888889e-03, 4.1666666666666667e-02, -0.5):
        p = p * s + c
    return 1.0 + s * p


def transmission(delta, beta):
    turn = (delta - 0.5) * np.float32(np.pi)
    amp = jnp.exp(-beta)
    return jnp.concatenate([-amp * sin_poly(turn), -amp * cos_poly(turn)], axis=0)


def pick(index, values):
    out = values[0]
    for i in range(1, len(values)):
        out = jnp.where(index == i, values[i], out)
    return out


def prepare_kernel(order, depth, incident, delta, beta, *outs):
    @pl.when(depth[0] == 0)
    def _():
        for slot in range(VIEWS):
            view = order[slot]
            entering = jnp.concatenate([incident[0, view], incident[1, view]], axis=0)
            outs[slot][...] = times(transmission(delta[view, 0], beta[view, 0]), entering)
            outs[VIEWS + slot][...] = transmission(delta[view, 1], beta[view, 1])

    @pl.when(depth[0] > 0)
    def _():
        for m in range(VIEWS):
            view = order[lax.rem(depth[0] + 5 - m, 3)]
            for half in range(2):
                outs[2 * VIEWS + m][half] = transmission(delta[view, half], beta[view, half])


def first_kernel(a, b, c, chi, clo, out):
    out[...] = column_blur(a[...] + b[...] + c[...], chi[...], clo[...])


def middle_kernel(slab_end, half, which, inner, own, outer, *refs):
    trans, (rhi, rlo, chi, clo), outs = refs[:VIEWS], refs[VIEWS : VIEWS + 4], refs[VIEWS + 4 :]
    field = row_blur(inner[...], own[...], outer[...], rhi[...], rlo[...])
    if slab_end:
        outs[1][...] = field
    t = pick(which[0], [r[...] if half is None else r[half] for r in trans])
    outs[0][...] = column_blur(times(t, field), chi[...], clo[...])


def last_kernel(inner, own, outer, rhi, rlo, out):
    out[...] = row_blur(inner[...], own[...], outer[...], rhi[...], rlo[...])


def assemble_kernel(depth, *refs):
    early, late, out = refs[:VIEWS], refs[VIEWS : 2 * VIEWS], refs[2 * VIEWS]
    for slot in range(VIEWS):
        value = late[slot][...] + pick(lax.rem(depth[0] + 3 - slot, 3), [r[...] for r in early])
        out[0, slot, 0] = value[:ROWS]
        out[1, slot, 0] = value[ROWS:]


FIELD = jax.ShapeDtypeStruct((2 * ROWS, COLS), jnp.float32)
PAIR = jax.ShapeDtypeStruct((2, 2 * ROWS, COLS), jnp.float32)


def call(kernel, out_shape, args, scalars=0, hbm=(), out_hbm=False):
    vmem, smem = pl.BlockSpec(memory_space=pltpu.VMEM), pl.BlockSpec(memory_space=pltpu.SMEM)
    specs, held = [], []
    for i, arg in enumerate(args):
        scalar = i < scalars
        specs.append(smem if scalar else vmem)
        held.append(arg if scalar or i in hbm else pltpu.with_memory_space_constraint(arg, pltpu.VMEM))
    shapes = out_shape if out_hbm else jax.tree.map(lambda s: pltpu.VMEM(s.shape, s.dtype), out_shape)
    return pl.pallas_call(
        kernel, out_shape=shapes, in_specs=specs, out_specs=jax.tree.map(lambda _: vmem, out_shape)
    )(*held)


def permute(value, pairs):
    return lax.ppermute(value, AXES, pairs)


def propagate(incident, delta, beta, view_order):
    depth, tile = lax.axis_index("depth"), lax.axis_index("tile")
    chip_z, x_lo = tile % 8, tile // 32
    slot = jnp.minimum((depth // 2) * 2 + chip_z // 4, VIEWS - 1)
    row_z = jnp.where(depth % 2 == 0, chip_z, 7 - chip_z)
    row_y = jnp.where(x_lo == 0, tile % 32 // 8, 3 - tile % 32 // 8)
    place = x_lo * 32 + row_y * 8 + row_z

    chi, clo = halves(column_matrix())
    even, odd = row_matrix(0), row_matrix(1)
    edge = jnp.logical_or(place == 0, place == TILES - 1)
    keep = jnp.logical_or(jnp.logical_not(edge), jnp.arange(6 * ROWS)[None, :] < 4 * ROWS)
    (ehi, elo), (ohi, olo) = halves(even), halves(odd)
    rhi = jnp.where(keep, jnp.where(place % 2 == 0, ehi, ohi), 0)
    rlo = jnp.where(keep, jnp.where(place % 2 == 0, elo, olo), 0)

    sent = call(
        prepare_kernel,
        [FIELD] * (2 * VIEWS) + [PAIR] * VIEWS,
        (view_order, depth[None], incident, delta, beta),
        scalars=2,
        hbm=(2, 3, 4),
    )
    entering, second, rest = sent[:VIEWS], sent[VIEWS : 2 * VIEWS], sent[2 * VIEWS :]

    def from_first(values):
        return [permute(values[k], [(home(0, p), worker(k, p)) for p in range(TILES)]) for k in range(VIEWS)]

    starts = from_first(entering)
    seconds = from_first(second)
    later = [
        permute(rest[m], [(home(1 + (m + k) % 3, p), worker(k, p)) for k in range(VIEWS) for p in range(TILES)])
        for m in range(3)
    ]
    own = call(first_kernel, FIELD, (*starts, chi, clo))
    slabs = []
    for piece in range(2 * SLABS):
        inner = permute(own, INNER)
        outer = permute(own, OUTER)
        if piece == 2 * SLABS - 1:
            slabs.append(call(last_kernel, FIELD, (inner, own, outer, rhi, rlo)))
            break
        slab_end = piece % 2 == 1
        nxt = piece + 1
        if nxt == 1:
            t, half, which = seconds, None, slot
        else:
            t, half, which = later, nxt % 2, (nxt // 2 + 5 - slot) % 3
        outs = call(
            functools.partial(middle_kernel, slab_end, half),
            [FIELD] * (2 if slab_end else 1),
            (which[None], inner, own, outer, *t, rhi, rlo, chi, clo),
            scalars=1,
        )
        own = outs[0]
        if slab_end:
            slabs.append(outs[1])

    early = [
        permute(
            pick((slot + n) % 3, slabs[:3]),
            [(worker(k, p), home((n + k) % 3, p)) for k in range(VIEWS) for p in range(TILES)],
        )
        for n in range(3)
    ]
    late = [permute(slabs[3], [(worker(k, p), home(SLABS - 1, p)) for p in range(TILES)]) for k in range(VIEWS)]
    shape = jax.ShapeDtypeStruct((2, VIEWS, 1, ROWS, COLS), jnp.float32)
    return call(assemble_kernel, shape, (depth[None], *early, *late), scalars=1, out_hbm=True)


def solution(mesh):
    return jax.shard_map(
        propagate,
        mesh=mesh,
        in_specs=(
            P(None, None, "tile", None),
            P(None, "depth", "tile", None),
            P(None, "depth", "tile", None),
            P(),
        ),
        out_specs=P(None, None, "depth", "tile", None),
        check_vma=False,
    )
```

```python
import functools

import jax
import jax.numpy as jnp
import numpy as np
from jax import lax
from jax.experimental import pallas as pl
from jax.experimental.pallas import tpu as pltpu
from jax.sharding import PartitionSpec as P

HALF = 32
ROWS = 32
COLS = 512
LANES = 128
VIEWS = 3
SLABS = 4
TILES = 64
AXES = ("depth", "tile")


def device_at(x, y, z, core):
    return ((x // 2) * 2 + core) * TILES + (x % 2) * 32 + y * 8 + z


def flipped(slot):
    return 1 - slot % 2


def worker(slot, tile):
    x_lo, rest = divmod(tile, 32)
    y, z = divmod(rest, 8)
    y = 3 - y if x_lo == flipped(slot) else y
    core = 0 if z // 4 == slot % 2 else 1
    return device_at(2 * (slot // 2) + x_lo, y, z if core == 0 else 7 - z, core)


def home(depth, tile):
    return depth * TILES + tile


def place_of(device):
    depth, tile = divmod(device, TILES)
    return 2 * (depth // 2) + tile // 32, tile % 32 // 8, tile % 8, depth % 2


def distance(a, b):
    (ax, ay, az, ac), (bx, by, bz, bc) = place_of(a), place_of(b)
    hops = [min((p - q) % n, (q - p) % n) for p, q, n in ((ax, bx, 4), (ay, by, 4), (az, bz, 8))]
    return 4 * sum(hops) + abs(ac - bc)


def completed(pairs):
    sources = sorted(set(range(SLABS * TILES)) - {a for a, _ in pairs})
    targets = sorted(set(range(SLABS * TILES)) - {b for _, b in pairs})
    extra = []
    for a, b in sorted(((a, b) for a in sources for b in targets), key=lambda ab: (distance(*ab), ab)):
        if a in sources and b in targets:
            sources.remove(a)
            targets.remove(b)
            extra.append((a, b))
    return list(pairs) + extra


INNER = [(worker(k, p), worker(k, p ^ 1)) for k in range(4) for p in range(TILES)]
OUTER = [
    (worker(k, p), worker(k, (p + 1 if p % 2 else p - 1) % TILES))
    for k in range(4)
    for p in range(TILES)
]


GIVES = [
    {0: 0, 1: 1},
    {1: 0, 2: 1},
    {2: 0, 0: 1, 1: 2},
    {0: 3, 2: 2},
    {1: 3, 0: 2},
    {2: 3},
]
FIRST = [0, 1]


def ready(slab):
    return [give for give in GIVES if max(give.values()) == slab]


def taps():
    grid = np.arange(-HALF, HALF + 1).astype(np.float64)
    value = (0.75 + 0.25 * np.cos(np.pi * grid / (HALF + 1))) * np.exp(1j * np.pi * grid * grid / (6.25 * HALF))
    return value / np.abs(value.sum())


def tap_at(offset):
    table = taps()
    inside = np.abs(offset) <= HALF
    return np.where(inside, table[np.clip(offset + HALF, 0, 2 * HALF)], 0.0)


def halves(matrix):
    matrix = jnp.asarray(matrix.astype(np.float32))
    high = matrix.astype(jnp.bfloat16)
    low = (matrix - high.astype(jnp.float32)).astype(jnp.bfloat16)
    return high, low


def column_matrix():
    source = np.arange(3 * LANES)[:, None] - LANES
    target = np.arange(LANES)[None, :]
    value = tap_at(source - target)
    return np.concatenate([value.real, value.imag], axis=1)


def row_block(shift):
    target = np.arange(ROWS)[:, None]
    source = np.arange(ROWS)[None, :] + shift
    value = tap_at(source - target)
    return np.block([[value.real, -value.imag], [value.imag, value.real]])


def row_matrix(parity):
    low, mid, high = row_block(-ROWS), row_block(0), row_block(ROWS)
    first, last = (low, high) if parity else (high, low)
    return np.concatenate([first, mid, last], axis=1)


def split(value):
    high = value.astype(jnp.bfloat16)
    return high, (value - high.astype(jnp.float32)).astype(jnp.bfloat16)


def dot(a, b):
    return jnp.dot(a, b, preferred_element_type=jnp.float32)


def row_blur(inner, own, outer, rhi, rlo):
    high, low = split(jnp.concatenate([inner, own, outer], axis=0))
    return dot(rhi, high) + (dot(rlo, high) + dot(rhi, low))


def column_blur(field, chi, clo):
    high, low = split(field)
    parts = []
    for b in range(COLS // LANES):
        first, last = max(0, b - 1), min(COLS // LANES, b + 2)
        cols = slice(first * LANES, last * LANES)
        rows = slice((first - b + 1) * LANES, (last - b + 1) * LANES)
        h, l = high[:, cols], low[:, cols]
        ch, cl = chi[rows], clo[rows]
        out = dot(h, ch) + (dot(l, ch) + dot(h, cl))
        real = out[:ROWS, :LANES] - out[ROWS:, LANES:]
        imag = out[:ROWS, LANES:] + out[ROWS:, :LANES]
        parts.append(jnp.concatenate([real, imag], axis=0))
    return jnp.concatenate(parts, axis=1)


def times(trans, field):
    tr, ti = trans[:ROWS], trans[ROWS:]
    fr, fi = field[:ROWS], field[ROWS:]
    return jnp.concatenate([fr * tr - fi * ti, fr * ti + fi * tr], axis=0)


def sin_poly(x):
    s = x * x
    p = -2.5052108385441720e-08
    for c in (2.7557319223985893e-06, -1.9841269841269841e-04, 8.3333333333333333e-03, -1.6666666666666667e-01):
        p = p * s + c
    return x + x * (s * p)


def cos_poly(x):
    s = x * x
    p = 2.0876756987868099e-09
    for c in (-2.7557319223985888e-07, 2.4801587301587302e-05, -1.3888888888888889e-03, 4.1666666666666667e-02, -0.5):
        p = p * s + c
    return 1.0 + s * p


def transmission(delta, beta):
    turn = (delta - 0.5) * np.float32(np.pi)
    amp = jnp.exp(-beta)
    return jnp.concatenate([-amp * sin_poly(turn), -amp * cos_poly(turn)], axis=0)


def pick(index, values):
    out = values[0]
    for i in range(1, len(values)):
        out = jnp.where(index == i, values[i], out)
    return out


def turn(slot):
    return (slot + 1) % VIEWS


def prepare_kernel(order, depth, incident, delta, beta, *outs):
    for m in range(SLABS):
        step = lax.rem(m + SLABS - depth[0], SLABS)

        @pl.when(step < VIEWS)
        def _(m=m, step=step):
            view = order[lax.rem(step + VIEWS - 1, VIEWS)]
            first = transmission(delta[view, 0], beta[view, 0])
            outs[m][0] = first
            outs[m][1] = transmission(delta[view, 1], beta[view, 1])

            @pl.when(depth[0] == 0)
            def _():
                entering = jnp.concatenate([incident[0, view], incident[1, view]], axis=0)
                outs[m][0] = times(first, entering)
                for n, k in enumerate(FIRST):
                    if turn(k) == m:
                        outs[SLABS + n][...] = times(first, entering)


def first_kernel(slot, *refs):
    fields, (chi, clo, out) = refs[:VIEWS], refs[VIEWS:]
    field = pick(slot[0], [f[...] if k in FIRST else f[0] for k, f in enumerate(fields)])
    out[...] = column_blur(field, chi[...], clo[...])


def give_out(which, slabs, outs):
    for give, out in zip(ready(len(slabs) - 1), outs, strict=True):
        some = next(iter(give.values()))
        out[...] = pick(which, [slabs[give.get(k, some)] for k in range(VIEWS)])


def middle_kernel(piece, slot, inner, own, outer, *refs):
    slab_end = piece % 2 == 1
    nxt = piece + 1
    done = piece // 2 if slab_end else 0
    older, refs = refs[:done], refs[done:]
    trans, (rhi, rlo, chi, clo), outs = refs[:SLABS], refs[SLABS : SLABS + 4], refs[SLABS + 4 :]
    field = row_blur(inner[...], own[...], outer[...], rhi[...], rlo[...])
    which = lax.rem(lax.rem(slot[0] + 1, VIEWS) + nxt // 2, SLABS)
    t = pick(which, [r[nxt % 2] for r in trans])
    outs[0][...] = column_blur(times(t, field), chi[...], clo[...])
    if slab_end:
        outs[1][...] = field
        give_out(slot[0], [r[...] for r in older] + [field], outs[2:])


def last_kernel(which, inner, own, outer, *refs):
    older, (rhi, rlo), outs = refs[: SLABS - 1], refs[SLABS - 1 : SLABS + 1], refs[SLABS + 1 :]
    field = row_blur(inner[...], own[...], outer[...], rhi[...], rlo[...])
    give_out(which[0], [r[...] for r in older] + [field], outs)


FIELD = jax.ShapeDtypeStruct((2 * ROWS, COLS), jnp.float32)
PAIR = jax.ShapeDtypeStruct((2, 2 * ROWS, COLS), jnp.float32)


def assemble_kernel(depth, *refs):
    received, out = refs[:-1], refs[-1]
    for j in range(SLABS):

        @pl.when(depth[0] == j)
        def _():
            for k in range(VIEWS):
                (n,) = [n for n, give in enumerate(GIVES) if give.get(k) == j]
                value = received[n][...]
                out[0, k, 0] = value[:ROWS]
                out[1, k, 0] = value[ROWS:]


def call(kernel, out_shape, args, scalars=0, hbm=(), out_hbm=False, grant=16 << 20):
    vmem, smem = pl.BlockSpec(memory_space=pltpu.VMEM), pl.BlockSpec(memory_space=pltpu.SMEM)
    specs, held = [], []
    for i, arg in enumerate(args):
        scalar = i < scalars
        specs.append(smem if scalar else vmem)
        held.append(arg if scalar or i in hbm else pltpu.with_memory_space_constraint(arg, pltpu.VMEM))
    shapes = out_shape if out_hbm else jax.tree.map(lambda s: pltpu.VMEM(s.shape, s.dtype), out_shape)
    return pl.pallas_call(
        kernel,
        out_shape=shapes,
        in_specs=specs,
        out_specs=jax.tree.map(lambda _: vmem, out_shape),
        compiler_params=pltpu.CompilerParams(vmem_limit_bytes=grant),
    )(*held)


def permute(value, pairs):
    return lax.ppermute(value, AXES, pairs)


def propagate(incident, delta, beta, view_order):
    depth, tile = lax.axis_index("depth"), lax.axis_index("tile")
    chip_z, x_lo = tile % 8, tile // 32
    quarter = (depth // 2) * 2 + chip_z // 4
    slot = jnp.minimum(quarter, VIEWS - 1)
    row_z = jnp.where(depth % 2 == 0, chip_z, 7 - chip_z)
    row_y = jnp.where(x_lo == flipped(quarter), 3 - tile % 32 // 8, tile % 32 // 8)
    place = x_lo * 32 + row_y * 8 + row_z

    chi, clo = halves(column_matrix())
    even, odd = row_matrix(0), row_matrix(1)
    edge = jnp.logical_or(place == 0, place == TILES - 1)
    keep = jnp.logical_or(jnp.logical_not(edge), jnp.arange(6 * ROWS)[None, :] < 4 * ROWS)
    (ehi, elo), (ohi, olo) = halves(even), halves(odd)
    rhi = jnp.where(keep, jnp.where(place % 2 == 0, ehi, ohi), 0)
    rlo = jnp.where(keep, jnp.where(place % 2 == 0, elo, olo), 0)

    rest = call(
        prepare_kernel,
        [PAIR] * SLABS + [FIELD] * len(FIRST),
        (view_order, depth[None], incident, delta, beta),
        scalars=2,
        hbm=(2, 3, 4),
        grant=None,
    )
    trans = []
    for m in range(SLABS):
        pairs = [(home((m - turn(k)) % SLABS, p), worker(k, p)) for k in range(VIEWS) for p in range(TILES)]
        trans.append(permute(rest[m], completed(pairs)))

    fields = [trans[turn(k)] for k in range(VIEWS)]
    for k, value in zip(FIRST, rest[SLABS:]):
        fields[k] = permute(value, [(home(0, p), worker(k, p)) for p in range(TILES)])

    own = call(first_kernel, FIELD, (slot[None], *fields, chi, clo), scalars=1)
    slabs, received = [], []
    for piece in range(2 * SLABS):
        inner = permute(own, INNER)
        outer = permute(own, OUTER)
        nxt = piece + 1
        if nxt < 2 * SLABS:
            leaving = len(ready(piece // 2)) if piece % 2 else -1
            outs = call(
                functools.partial(middle_kernel, piece),
                [FIELD] * (2 + leaving),
                (slot[None], inner, own, outer, *(slabs if piece % 2 else ()), *trans, rhi, rlo, chi, clo),
                scalars=1,
            )
            own, outs = outs[0], outs[1:]
            if piece % 2:
                slabs.append(outs[0])
                outs = outs[1:]
        else:
            outs = call(
                last_kernel,
                [FIELD] * len(ready(SLABS - 1)),
                (slot[None], inner, own, outer, *slabs, rhi, rlo),
                scalars=1,
            )
        for value in outs:
            n = len(received)
            pairs = [(worker(k, p), home(j, p)) for k, j in GIVES[n].items() for p in range(TILES)]
            received.append(permute(value, completed(pairs)))
    shape = jax.ShapeDtypeStruct((2, VIEWS, 1, ROWS, COLS), jnp.float32)
    return call(assemble_kernel, shape, (depth[None], *received), scalars=1, out_hbm=True)


def solution(mesh):
    return jax.shard_map(
        propagate,
        mesh=mesh,
        in_specs=(
            P(None, None, "tile", None),
            P(None, "depth", "tile", None),
            P(None, "depth", "tile", None),
            P(),
        ),
        out_specs=P(None, None, "depth", "tile", None),
        check_vma=False,
    )
```

```python
import functools

import jax
import jax.numpy as jnp
import numpy as np
from jax import lax
from jax.experimental import pallas as pl
from jax.experimental.pallas import tpu as pltpu
from jax.sharding import PartitionSpec as P

HALF = 32
ROWS = 32
COLS = 512
LANES = 128
VIEWS = 3
SLABS = 4
TILES = 64
AXES = ("depth", "tile")


def device_at(x, y, z, core):
    return ((x // 2) * 2 + core) * TILES + (x % 2) * 32 + y * 8 + z


def flipped(slot):
    return 1 - slot % 2


def worker(slot, tile):
    x_lo, rest = divmod(tile, 32)
    y, z = divmod(rest, 8)
    y = 3 - y if x_lo == flipped(slot) else y
    core = 0 if z // 4 == slot % 2 else 1
    return device_at(2 * (slot // 2) + x_lo, y, z if core == 0 else 7 - z, core)


def home(depth, tile):
    return depth * TILES + tile


def place_of(device):
    depth, tile = divmod(device, TILES)
    return 2 * (depth // 2) + tile // 32, tile % 32 // 8, tile % 8, depth % 2


def distance(a, b):
    (ax, ay, az, ac), (bx, by, bz, bc) = place_of(a), place_of(b)
    hops = [min((p - q) % n, (q - p) % n) for p, q, n in ((ax, bx, 4), (ay, by, 4), (az, bz, 8))]
    return 4 * sum(hops) + abs(ac - bc)


def completed(pairs):
    sources = sorted(set(range(SLABS * TILES)) - {a for a, _ in pairs})
    targets = sorted(set(range(SLABS * TILES)) - {b for _, b in pairs})
    extra = []
    for a, b in sorted(((a, b) for a in sources for b in targets), key=lambda ab: (distance(*ab), ab)):
        if a in sources and b in targets:
            sources.remove(a)
            targets.remove(b)
            extra.append((a, b))
    return list(pairs) + extra


INNER = [(worker(k, p), worker(k, p ^ 1)) for k in range(4) for p in range(TILES)]
OUTER = [
    (worker(k, p), worker(k, (p + 1 if p % 2 else p - 1) % TILES))
    for k in range(4)
    for p in range(TILES)
]


GIVES = [
    {0: 0, 1: 1},
    {1: 0, 2: 1},
    {2: 0, 0: 1, 1: 2},
    {0: 3, 2: 2},
    {1: 3, 0: 2},
    {2: 3},
]
SENDS = [{2: 0, 0: 3, 1: 2}, {2: 1, 0: 0, 1: 3}, {2: 2, 0: 1, 1: 0}, {2: 3, 0: 2, 1: 1}]
FULL = [0, 1, 2, 3]
FIRST = [1]


def ready(slab):
    return [give for give in GIVES if max(give.values()) == slab]


def taps():
    grid = np.arange(-HALF, HALF + 1).astype(np.float64)
    value = (0.75 + 0.25 * np.cos(np.pi * grid / (HALF + 1))) * np.exp(1j * np.pi * grid * grid / (6.25 * HALF))
    return value / np.abs(value.sum())


def tap_at(offset):
    table = taps()
    inside = np.abs(offset) <= HALF
    return np.where(inside, table[np.clip(offset + HALF, 0, 2 * HALF)], 0.0)


def halves(matrix):
    matrix = jnp.asarray(matrix.astype(np.float32))
    high = matrix.astype(jnp.bfloat16)
    low = (matrix - high.astype(jnp.float32)).astype(jnp.bfloat16)
    return high, low


def column_matrix():
    source = np.arange(3 * LANES)[:, None] - LANES
    target = np.arange(LANES)[None, :]
    value = tap_at(source - target)
    return np.concatenate([value.real, value.imag], axis=1)


def row_block(shift):
    target = np.arange(ROWS)[:, None]
    source = np.arange(ROWS)[None, :] + shift
    value = tap_at(source - target)
    return np.block([[value.real, -value.imag], [value.imag, value.real]])


def row_matrix(parity):
    low, mid, high = row_block(-ROWS), row_block(0), row_block(ROWS)
    first, last = (low, high) if parity else (high, low)
    return np.concatenate([first, mid, last], axis=1)


def split(value):
    high = value.astype(jnp.bfloat16)
    return high, (value - high.astype(jnp.float32)).astype(jnp.bfloat16)


def dot(a, b):
    return jnp.dot(a, b, preferred_element_type=jnp.float32)


def row_blur(inner, own, outer, rhi, rlo):
    high, low = split(jnp.concatenate([inner, own, outer], axis=0))
    return dot(rhi, high) + (dot(rlo, high) + dot(rhi, low))


def column_blur(field, chi, clo):
    high, low = split(field)
    parts = []
    for b in range(COLS // LANES):
        first, last = max(0, b - 1), min(COLS // LANES, b + 2)
        cols = slice(first * LANES, last * LANES)
        rows = slice((first - b + 1) * LANES, (last - b + 1) * LANES)
        h, l = high[:, cols], low[:, cols]
        ch, cl = chi[rows], clo[rows]
        out = dot(h, ch) + (dot(l, ch) + dot(h, cl))
        real = out[:ROWS, :LANES] - out[ROWS:, LANES:]
        imag = out[:ROWS, LANES:] + out[ROWS:, :LANES]
        parts.append(jnp.concatenate([real, imag], axis=0))
    return jnp.concatenate(parts, axis=1)


def times(trans, field):
    tr, ti = trans[:ROWS], trans[ROWS:]
    fr, fi = field[:ROWS], field[ROWS:]
    return jnp.concatenate([fr * tr - fi * ti, fr * ti + fi * tr], axis=0)


def sin_poly(x):
    s = x * x
    p = -2.5052108385441720e-08
    for c in (2.7557319223985893e-06, -1.9841269841269841e-04, 8.3333333333333333e-03, -1.6666666666666667e-01):
        p = p * s + c
    return x + x * (s * p)


def cos_poly(x):
    s = x * x
    p = 2.0876756987868099e-09
    for c in (-2.7557319223985888e-07, 2.4801587301587302e-05, -1.3888888888888889e-03, 4.1666666666666667e-02, -0.5):
        p = p * s + c
    return 1.0 + s * p


def transmission(delta, beta):
    turn = (delta - 0.5) * np.float32(np.pi)
    amp = jnp.exp(-beta)
    return jnp.concatenate([-amp * sin_poly(turn), -amp * cos_poly(turn)], axis=0)


def pick(index, values):
    out = values[0]
    for i in range(1, len(values)):
        out = jnp.where(index == i, values[i], out)
    return out


def send_of(slot, slab):
    (m,) = [m for m, send in enumerate(SENDS) if send.get(slot) == slab]
    return m


def prepare_kernel(order, depth, incident, delta, beta, *outs):
    for m, send in enumerate(SENDS):
        slot, active = 0, depth[0] < 0
        for k, d in send.items():
            slot = jnp.where(depth[0] == d, k, slot)
            active = jnp.logical_or(active, depth[0] == d)

        @pl.when(active)
        def _(m=m, slot=slot, send=send):
            view = order[slot]
            first = transmission(delta[view, 0], beta[view, 0])
            outs[m][0] = first
            outs[m][1] = transmission(delta[view, 1], beta[view, 1])
            if 0 in send.values():

                @pl.when(depth[0] == 0)
                def _():
                    entering = jnp.concatenate([incident[0, view], incident[1, view]], axis=0)
                    outs[m][0] = times(first, entering)
                    for n, k in enumerate(FIRST):
                        if send.get(k) == 0:
                            outs[len(SENDS) + n][...] = times(first, entering)


def first_kernel(slot, *refs):
    fields, (chi, clo, out) = refs[:VIEWS], refs[VIEWS:]
    field = pick(slot[0], [f[...] if k in FIRST else f[0] for k, f in enumerate(fields)])
    out[...] = column_blur(field, chi[...], clo[...])


def give_out(which, slabs, outs):
    for give, out in zip(ready(len(slabs) - 1), outs, strict=True):
        some = next(iter(give.values()))
        out[...] = pick(which, [slabs[give.get(k, some)] for k in range(VIEWS)])


def middle_kernel(piece, slot, inner, own, outer, *refs):
    slab_end = piece % 2 == 1
    nxt = piece + 1
    done = piece // 2 if slab_end else 0
    older, refs = refs[:done], refs[done:]
    trans, (rhi, rlo, chi, clo), outs = refs[:VIEWS], refs[VIEWS : VIEWS + 4], refs[VIEWS + 4 :]
    field = row_blur(inner[...], own[...], outer[...], rhi[...], rlo[...])
    t = pick(slot[0], [r[nxt % 2] for r in trans])
    outs[0][...] = column_blur(times(t, field), chi[...], clo[...])
    if slab_end:
        outs[1][...] = field
        give_out(slot[0], [r[...] for r in older] + [field], outs[2:])


def last_kernel(which, inner, own, outer, *refs):
    older, (rhi, rlo), outs = refs[: SLABS - 1], refs[SLABS - 1 : SLABS + 1], refs[SLABS + 1 :]
    field = row_blur(inner[...], own[...], outer[...], rhi[...], rlo[...])
    give_out(which[0], [r[...] for r in older] + [field], outs)


FIELD = jax.ShapeDtypeStruct((2 * ROWS, COLS), jnp.float32)
PAIR = jax.ShapeDtypeStruct((2, 2 * ROWS, COLS), jnp.float32)


def assemble_kernel(depth, *refs):
    received, out = refs[:-1], refs[-1]
    for j in range(SLABS):

        @pl.when(depth[0] == j)
        def _():
            for k in range(VIEWS):
                (n,) = [n for n, give in enumerate(GIVES) if give.get(k) == j]
                value = received[n][...]
                out[0, k, 0] = value[:ROWS]
                out[1, k, 0] = value[ROWS:]


def call(kernel, out_shape, args, scalars=0, hbm=(), out_hbm=False, grant=16 << 20):
    vmem, smem = pl.BlockSpec(memory_space=pltpu.VMEM), pl.BlockSpec(memory_space=pltpu.SMEM)
    specs, held = [], []
    for i, arg in enumerate(args):
        scalar = i < scalars
        specs.append(smem if scalar else vmem)
        held.append(arg if scalar or i in hbm else pltpu.with_memory_space_constraint(arg, pltpu.VMEM))
    shapes = out_shape if out_hbm else jax.tree.map(lambda s: pltpu.VMEM(s.shape, s.dtype), out_shape)
    return pl.pallas_call(
        kernel,
        out_shape=shapes,
        in_specs=specs,
        out_specs=jax.tree.map(lambda _: vmem, out_shape),
        compiler_params=pltpu.CompilerParams(vmem_limit_bytes=grant),
    )(*held)


def permute(value, pairs):
    return lax.ppermute(value, AXES, pairs)


def propagate(incident, delta, beta, view_order):
    depth, tile = lax.axis_index("depth"), lax.axis_index("tile")
    chip_z, x_lo = tile % 8, tile // 32
    quarter = (depth // 2) * 2 + chip_z // 4
    slot = jnp.minimum(quarter, VIEWS - 1)
    row_z = jnp.where(depth % 2 == 0, chip_z, 7 - chip_z)
    row_y = jnp.where(x_lo == flipped(quarter), 3 - tile % 32 // 8, tile % 32 // 8)
    place = x_lo * 32 + row_y * 8 + row_z

    chi, clo = halves(column_matrix())
    even, odd = row_matrix(0), row_matrix(1)
    edge = jnp.logical_or(place == 0, place == TILES - 1)
    keep = jnp.logical_or(jnp.logical_not(edge), jnp.arange(6 * ROWS)[None, :] < 4 * ROWS)
    (ehi, elo), (ohi, olo) = halves(even), halves(odd)
    rhi = jnp.where(keep, jnp.where(place % 2 == 0, ehi, ohi), 0)
    rlo = jnp.where(keep, jnp.where(place % 2 == 0, elo, olo), 0)

    rest = call(
        prepare_kernel,
        [PAIR] * len(SENDS) + [FIELD] * len(FIRST),
        (view_order, depth[None], incident, delta, beta),
        scalars=2,
        hbm=(2, 3, 4),
        grant=None,
    )
    trans = []
    for m, send in enumerate(SENDS):
        pairs = [(home(d, p), worker(k, p)) for k, d in send.items() for p in range(TILES)]
        trans.append(permute(rest[m], completed(pairs) if m in FULL else pairs))
    fields = [trans[send_of(k, 0)] for k in range(VIEWS)]
    for k, value in zip(FIRST, rest[len(SENDS) :]):
        fields[k] = permute(value, completed([(home(0, p), worker(k, p)) for p in range(TILES)]))

    own = call(first_kernel, FIELD, (slot[None], *fields, chi, clo), scalars=1)
    slabs, received = [], []
    for piece in range(2 * SLABS):
        inner = permute(own, INNER)
        outer = permute(own, OUTER)
        nxt = piece + 1
        if nxt < 2 * SLABS:
            here = [trans[send_of(k, nxt // 2)] for k in range(VIEWS)]
            leaving = len(ready(piece // 2)) if piece % 2 else -1
            outs = call(
                functools.partial(middle_kernel, piece),
                [FIELD] * (2 + leaving),
                (slot[None], inner, own, outer, *(slabs if piece % 2 else ()), *here, rhi, rlo, chi, clo),
                scalars=1,
            )
            own, outs = outs[0], outs[1:]
            if piece % 2:
                slabs.append(outs[0])
                outs = outs[1:]
        else:
            outs = call(
                last_kernel,
                [FIELD] * len(ready(SLABS - 1)),
                (slot[None], inner, own, outer, *slabs, rhi, rlo),
                scalars=1,
            )
        for value in outs:
            n = len(received)
            pairs = [(worker(k, p), home(j, p)) for k, j in GIVES[n].items() for p in range(TILES)]
            received.append(permute(value, completed(pairs)))
    shape = jax.ShapeDtypeStruct((2, VIEWS, 1, ROWS, COLS), jnp.float32)
    return call(assemble_kernel, shape, (depth[None], *received), scalars=1, out_hbm=True)


def solution(mesh):
    return jax.shard_map(
        propagate,
        mesh=mesh,
        in_specs=(
            P(None, None, "tile", None),
            P(None, "depth", "tile", None),
            P(None, "depth", "tile", None),
            P(),
        ),
        out_specs=P(None, None, "depth", "tile", None),
        check_vma=False,
    )
```
